32 devices in a mesh: section: 8 (over y, x, core), tensor: 4 (over z).
Axes of the slice: x: 2, y: 2, z: 4, core: 2. Of those that a mesh axis runs over, the one named last changes fastest.
Arguments:
- inputs_down: bfloat16 [8, 2, 240, 2048], P('section', None, 'tensor'), may hold values from -6 to 6
- inputs_up: bfloat16 [8, 2, 240, 2048], P('section', None, 'tensor'), may hold values from -6 to 6
- grads_down: bfloat16 [8, 240, 2048], P('section', 'tensor'), may hold values from -6 to 6
- grads_up: bfloat16 [8, 240, 2048], P('section', 'tensor'), may hold values from -6 to 6
- loss_grads: bfloat16 [2, 240, 2048], P(None, 'tensor'), may hold values from -6 to 6
- first_down: bfloat16 [8, 2048, 4096], P('section', None, 'tensor'), may hold values from -6 to 6
- second_down: bfloat16 [8, 4096, 2048], P('section', 'tensor'), may hold values from -6 to 6
- first_up: bfloat16 [8, 2048, 4096], P('section', None, 'tensor'), may hold values from -6 to 6
- second_up: bfloat16 [8, 4096, 2048], P('section', 'tensor'), may hold values from -6 to 6
- momentum_first: bfloat16 [8, 2048, 4096], P('section', None, 'tensor'), may hold values from -3 to 3
- momentum_second: bfloat16 [8, 4096, 2048], P('section', 'tensor'), may hold values from -3 to 3
Outputs:
- first_new: bfloat16 [8, 2048, 4096], P('section', None, 'tensor')
- second_new: bfloat16 [8, 4096, 2048], P('section', 'tensor')
- momentum_one: bfloat16 [8, 2048, 4096], P('section', None, 'tensor')
- momentum_two: bfloat16 [8, 4096, 2048], P('section', 'tensor')
- passed_down: bfloat16 [8, 240, 2048], P('section', 'tensor')
- passed_up: bfloat16 [8, 240, 2048], P('section', 'tensor')
The draws below stay inside these ranges and needn't reach their ends.
All inputs are finite; a program needn't handle non-finite values.
Results may differ from the reference program's by a relative error of at most 0.0063.
Values may be sent and summed in bfloat16 or wider, within the bound.
No kernel may reach another device: no remote copies, remote signals or barrier semaphores. Data moves between devices by JAX's collectives and lax.ppermute only.
A program may use at most 128 MiB of HBM per device.

```python
import jax
import jax.numpy as jnp
from jax import lax

D = 2048
FF = 4096
MB_TOK = 240
SECTIONS = 8


def block_levels(own_key, extent, split, low, high):
    factor_of, own = 1.0, jax.random.fold_in(own_key, 6)
    for axis_at, blocks in split:
        heights = jnp.exp(jax.random.uniform(jax.random.fold_in(own, axis_at), (blocks,), jnp.float32, low / len(split), high / len(split)))
        factor_of = factor_of * jnp.repeat(heights, extent[axis_at] // blocks).reshape([-1 if axis == axis_at else 1 for axis in range(len(extent))])
    return factor_of


def normal_values(own_key, dims, width, reach, shards=(), held_as=jnp.bfloat16):
    drawn = width * jax.random.normal(own_key, dims, jnp.float32)
    if shards:
        drawn = drawn * block_levels(own_key, dims, shards, -0.22, 0.18)
    return jnp.clip(drawn, -reach, reach).astype(held_as)


def setup_inputs(seed: int = 0) -> dict:
    splits = jax.random.split(jax.random.key(seed), 12)
    return {
        "inputs_down": normal_values(splits[0], (SECTIONS, 2, MB_TOK, D), 1.0, 6.0, ((0, 8), (2, 4))),
        "inputs_up": normal_values(splits[1], (SECTIONS, 2, MB_TOK, D), 1.0, 6.0, ((0, 8), (2, 4))),
        "grads_down": normal_values(splits[2], (SECTIONS, MB_TOK, D), 1.0, 6.0, ((0, 8), (1, 4))),
        "grads_up": normal_values(splits[3], (SECTIONS, MB_TOK, D), 1.0, 6.0, ((0, 8), (1, 4))),
        "loss_grads": normal_values(splits[4], (2, MB_TOK, D), 1.0, 6.0, ((1, 4),)),
        "first_down": normal_values(splits[5], (SECTIONS, D, FF), 1.0, 6.0, ((0, 8), (2, 4))),
        "second_down": normal_values(splits[6], (SECTIONS, FF, D), 1.0, 6.0, ((0, 8), (1, 4))),
        "first_up": normal_values(splits[7], (SECTIONS, D, FF), 1.0, 6.0, ((0, 8), (2, 4))),
        "second_up": normal_values(splits[8], (SECTIONS, FF, D), 1.0, 6.0, ((0, 8), (1, 4))),
        "momentum_first": normal_values(splits[9], (SECTIONS, D, FF), 0.5, 3.0, ((0, 8), (2, 4))),
        "momentum_second": normal_values(splits[10], (SECTIONS, FF, D), 0.5, 3.0, ((0, 8), (1, 4))),
    }


epsilon = 1e-05
learning_rate = 0.25
momentum_decay = 0.9
tanh_scale = 0.7978845608028654
cubic_term = 0.044715

def gelu_with_slope(preact):
    tanh_input = tanh_scale * (preact + cubic_term * preact * preact * preact)
    tangent = jnp.tanh(tanh_input)
    values = 0.5 * preact * (1.0 + tangent)
    slopes = 0.5 * (1.0 + tangent) + 0.5 * preact * (1.0 - tangent * tangent) * tanh_scale * (1.0 + 3.0 * cubic_term * preact * preact)
    return (values, slopes)

def normalize(inputs):
    widened = inputs.astype(jnp.float32)
    centred = widened - lax.optimization_barrier(jnp.mean(widened, axis=-1, keepdims=True))
    inverse_scale = lax.rsqrt(lax.optimization_barrier(jnp.mean(centred * centred, axis=-1, keepdims=True)) + epsilon)
    return (centred * inverse_scale, inverse_scale)

def contract_rows(left_side, right_side):
    return lax.dot_general(left_side, right_side, (((0,), (0,)), ((), ())), preferred_element_type=jnp.float32)

def contract_last(left_side, right_side):
    return lax.dot_general(left_side, right_side, (((1,), (1,)), ((), ())), preferred_element_type=jnp.float32)

def section_backward(inputs, cotangent, first_weight, second_weight):
    normed, inverse_scale = normalize(inputs)
    normed_low = normed.astype(jnp.bfloat16)
    preact = jnp.dot(normed_low, first_weight, preferred_element_type=jnp.float32) * D ** (-0.5)
    values, slopes = gelu_with_slope(preact)
    activation = values.astype(jnp.bfloat16)
    grad_activation = contract_last(cotangent, second_weight) * FF ** (-0.5)
    grad_preact = (grad_activation * slopes).astype(jnp.bfloat16)
    grad_normed = contract_last(grad_preact, first_weight) * D ** (-0.5)
    first_mean = lax.optimization_barrier(jnp.mean(grad_normed, axis=-1, keepdims=True))
    second_mean = lax.optimization_barrier(jnp.mean(grad_normed * normed, axis=-1, keepdims=True))
    grad_inputs = cotangent.astype(jnp.float32) + inverse_scale * (grad_normed - first_mean - normed * second_mean)
    grad_first = contract_rows(normed_low, grad_preact) * D ** (-0.5)
    grad_second = contract_rows(activation, cotangent) * FF ** (-0.5)
    return (grad_inputs.astype(jnp.bfloat16), (grad_first, grad_second))

def reference(inputs_down, inputs_up, grads_down, grads_up, loss_grads, first_down, second_down, first_up, second_up, momentum_first, momentum_second):
    weights = (first_down, second_down, first_up, second_up)

    def step_one(packed):
        passed_down, down_grads = section_backward(packed[0][0], packed[2], packed[4], packed[5])
        passed_up, up_grads = section_backward(packed[1][0], packed[3], packed[6], packed[7])
        return (passed_down, passed_up, down_grads, up_grads)
    one_down, one_up, down_one, up_one = lax.map(step_one, (inputs_down, inputs_up, grads_down, grads_up) + weights)
    cotan_down = jnp.concatenate([one_down[1:], loss_grads[0:1]], axis=0)
    cotan_up = jnp.concatenate([loss_grads[1:2], one_up[:-1]], axis=0)

    def step_two(packed):
        passed_down, down_grads = section_backward(packed[0][1], packed[2], packed[4], packed[5])
        passed_up, up_grads = section_backward(packed[1][1], packed[3], packed[6], packed[7])
        down_sums = (down_grads[0] + packed[8][0], down_grads[1] + packed[8][1])
        up_sums = ((up_grads[0] + packed[9][0]).astype(jnp.bfloat16), (up_grads[1] + packed[9][1]).astype(jnp.bfloat16))
        return (passed_down, passed_up, down_sums, up_sums)
    passed_down, passed_up, down_sums, up_sums = lax.map(step_two, (inputs_down, inputs_up, cotan_down, cotan_up) + weights + (down_one, up_one))
    total_first = down_sums[0] + up_sums[0][::-1].astype(jnp.float32)
    total_second = down_sums[1] + up_sums[1][::-1].astype(jnp.float32)
    moment_first = momentum_decay * momentum_first.astype(jnp.float32) + total_first
    moment_second = momentum_decay * momentum_second.astype(jnp.float32) + total_second
    first_new = (first_down.astype(jnp.float32) - learning_rate * moment_first).astype(jnp.bfloat16)
    second_new = (second_down.astype(jnp.float32) - learning_rate * moment_second).astype(jnp.bfloat16)
    return (first_new, second_new, moment_first.astype(jnp.bfloat16), moment_second.astype(jnp.bfloat16), passed_down, passed_up)
```

```python
import jax
import jax.numpy as jnp
from jax import lax
from jax.sharding import PartitionSpec as P

D = 2048
FF = 4096

epsilon = 1e-05
learning_rate = 0.25
momentum_decay = 0.9
tanh_scale = 0.7978845608028654
cubic_term = 0.044715
low = jnp.bfloat16
wide = jnp.float32


def shifted(value, by, first, last):
    return lax.ppermute(value, "tensor", [(i, i + by) for i in range(first, last)])


def gather_line(value):
    count = lax.axis_size("tensor")
    index = lax.axis_index("tensor")
    from_left, from_right = [value], [value]
    for step in range(1, count):
        from_left.append(shifted(from_left[-1], 1, step - 1, count - 1))
        from_right.append(shifted(from_right[-1], -1, 1, count - step + 1))
    return [value] + [
        jnp.where(index >= j, from_left[j], from_right[count - j]) for j in range(1, count)
    ]


def reduce_line(parts):
    count = lax.axis_size("tensor")
    total = parts[0]
    for by in (1, -1):
        carried = None
        for far in range(count - 1, 0, -1):
            own = parts[(-far * by) % count]
            if carried is not None:
                own = own + carried.astype(wide)
            first, last = (0, count - far) if by == 1 else (far, count)
            carried = shifted(own.astype(low), by, first, last)
        if carried is not None:
            total = total + carried.astype(wide)
    return total


def rotated(value, by):
    count = lax.axis_size("section")
    return lax.ppermute(value, "section", [(i, (i + by) % count) for i in range(count)])


def mirrored(value):
    count = lax.axis_size("section")
    return lax.ppermute(value, "section", [(i, count - 1 - i) for i in range(count)])


def gelu_with_slope(preact):
    tanh_input = tanh_scale * (preact + cubic_term * preact * preact * preact)
    tangent = jnp.tanh(tanh_input)
    values = 0.5 * preact * (1.0 + tangent)
    slopes = 0.5 * (1.0 + tangent) + 0.5 * preact * (1.0 - tangent * tangent) * tanh_scale * (
        1.0 + 3.0 * cubic_term * preact * preact
    )
    return (values, slopes)


def normalize(inputs):
    widened = inputs.astype(wide)
    centred = widened - jnp.mean(widened, axis=-1, keepdims=True)
    inverse_scale = lax.rsqrt(jnp.mean(centred * centred, axis=-1, keepdims=True) + epsilon)
    return (centred * inverse_scale, inverse_scale)


def contract_rows(left_side, right_side):
    return lax.dot_general(
        left_side, right_side, (((0,), (0,)), ((), ())), preferred_element_type=wide
    )


def contract_last(left_side, right_side):
    return lax.dot_general(
        left_side, right_side, (((1,), (1,)), ((), ())), preferred_element_type=wide
    )


def hidden_terms(normed_low, cotan, first, second):
    preact = jnp.dot(normed_low, first, preferred_element_type=wide) * D ** (-0.5)
    values, slopes = gelu_with_slope(preact)
    grad_activation = contract_last(cotan, second) * FF ** (-0.5)
    return values.astype(low), (grad_activation * slopes).astype(low)


def input_gradient(grad_normed, normed, inverse_scale, cotan):
    first_mean = jnp.mean(grad_normed, axis=-1, keepdims=True)
    second_mean = jnp.mean(grad_normed * normed, axis=-1, keepdims=True)
    return (
        cotan.astype(wide) + inverse_scale * (grad_normed - first_mean - normed * second_mean)
    ).astype(low)


def body(
    inputs_down,
    inputs_up,
    grads_down,
    grads_up,
    loss_grads,
    first_down,
    second_down,
    first_up,
    second_up,
    momentum_first,
    momentum_second,
):
    sections = lax.axis_size("section")
    position = lax.axis_index("section")
    count = lax.axis_size("tensor")
    rows = grads_down.shape[1]
    held = rows + (-rows) % 8

    def padded(value):
        return jnp.pad(value, ((0, held - rows), (0, 0)))

    firsts = (first_up[0], first_down[0])
    seconds = (second_up[0], second_down[0])
    inputs = (inputs_up[0], inputs_down[0])
    cotans = [padded(grads_up[0]), padded(grads_down[0])]
    losses = (padded(loss_grads[1]), padded(loss_grads[0]))
    edges = (sections - 1, 0)
    ways = (1, -1)
    normed = [[normalize(padded(inputs[b][s])) for s in range(2)] for b in range(2)]
    lows = [[normed[b][s][0].astype(low) for s in range(2)] for b in range(2)]
    kept = [[None, None], [None, None]]
    passed = [None, None]
    for step in range(2):
        for b in range(2):
            if step == 0:
                slots = gather_line(jnp.concatenate([lows[b][0], cotans[b]], axis=0))
                normed_low = jnp.concatenate([s[:held] for s in slots], axis=0)
                cotan = jnp.concatenate([s[held:] for s in slots], axis=0)
            else:
                normed_low = jnp.concatenate(gather_line(lows[b][1]), axis=0)
                cotan = jnp.concatenate(gather_line(cotans[b]), axis=0)
            activation, grad_preact = hidden_terms(normed_low, cotan, firsts[b], seconds[b])
            kept[b][step] = (normed_low, grad_preact, activation, cotan)
            partial = contract_last(grad_preact, firsts[b]) * D ** (-0.5)
            grad_normed = reduce_line([partial[j * held : (j + 1) * held] for j in range(count)])
            passed[b] = input_gradient(grad_normed, *normed[b][step], cotans[b])
            if step == 0:
                sent = jnp.where(position == edges[b], losses[b], passed[b])
                cotans[b] = rotated(sent, ways[b])
    mirror = [[mirrored(value) for value in kept[0][step]] for step in range(2)]

    def weight_terms(both):
        joined = [jnp.concatenate([both[0][i], both[1][i]], axis=0) for i in range(4)]
        return (
            contract_rows(joined[0], joined[1]) * D ** (-0.5),
            contract_rows(joined[2], joined[3]) * FF ** (-0.5),
        )

    down_terms = weight_terms(kept[1])
    mirror_terms = weight_terms(mirror)
    results = []
    for down, up, momentum, weight in zip(
        down_terms, mirror_terms, (momentum_first, momentum_second), (first_down, second_down)
    ):
        total = down + up.astype(low).astype(wide)
        moment = momentum_decay * momentum[0].astype(wide) + total
        fresh = (weight[0].astype(wide) - learning_rate * moment).astype(low)
        results.append((fresh, moment.astype(low)))
    return (
        results[0][0][None],
        results[1][0][None],
        results[0][1][None],
        results[1][1][None],
        passed[1][:rows][None],
        passed[0][:rows][None],
    )


def solution(mesh):
    placed = (
        P("section", None, "tensor", None),
        P("section", None, "tensor", None),
        P("section", "tensor", None),
        P("section", "tensor", None),
        P(None, "tensor", None),
        P("section", None, "tensor"),
        P("section", "tensor", None),
        P("section", None, "tensor"),
        P("section", "tensor", None),
        P("section", None, "tensor"),
        P("section", "tensor", None),
    )
    return jax.shard_map(
        body,
        mesh=mesh,
        in_specs=placed,
        out_specs=(
            P("section", None, "tensor"),
            P("section", "tensor", None),
            P("section", None, "tensor"),
            P("section", "tensor", None),
            P("section", "tensor", None),
            P("section", "tensor", None),
        ),
        check_vma=False,
    )
```

```python
import functools

import jax
import jax.numpy as jnp
from jax import lax
from jax.experimental import pallas as pl
from jax.experimental.pallas import tpu as pltpu
from jax.sharding import PartitionSpec as P


epsilon = 1e-05
learning_rate = 0.25
momentum_decay = 0.9
tanh_scale = 0.7978845608028654
cubic_term = 0.044715
low = jnp.bfloat16
wide = jnp.float32

NEAR = [(0, 1), (1, 0), (2, 3), (3, 2)]
MIDDLE = [(1, 2), (2, 1)]
OUTWARD = [(1, 0), (2, 3)]
INWARD = [(0, 1), (3, 2)]
SKIP = [(1, 3), (2, 0)]


def is_central():
    index = lax.axis_index("tensor")
    return (index == 1) | (index == 2)


def gather_line(value):
    count = lax.axis_size("tensor")
    if count == 4:
        near = lax.ppermute(value, "tensor", NEAR)
        inner = lax.ppermute(value, "tensor", MIDDLE)
        outer = lax.ppermute(near, "tensor", MIDDLE)
        inner_out = lax.ppermute(inner, "tensor", OUTWARD)
        outer_out = lax.ppermute(outer, "tensor", OUTWARD)
        return [value, near, (inner, inner_out), (outer, outer_out)]
    index = lax.axis_index("tensor")
    left, right = [value], [value]
    for step in range(1, count):
        ahead = [(i, i + 1) for i in range(step - 1, count - 1)]
        back = [(i + 1, i) for i in range(0, count - step)]
        left.append(lax.ppermute(left[-1], "tensor", ahead))
        right.append(lax.ppermute(right[-1], "tensor", back))
    return [value] + [jnp.where(index >= j, left[j], right[count - j]) for j in range(1, count)]


def chosen(slot):
    return jnp.where(is_central(), *slot) if isinstance(slot, tuple) else slot


def reduce_line(partial, beside, leaving):
    count = lax.axis_size("tensor")
    held = partial.shape[0] // count
    if count == 4:
        moved = lax.ppermute(leaving, "tensor", INWARD)
        near = lax.ppermute(beside, "tensor", NEAR)
        both = (partial[2 * held :] + moved.astype(wide)).astype(low)
        middle = lax.ppermute(both[:held], "tensor", MIDDLE)
        far = lax.ppermute(both[held:], "tensor", SKIP)
        total = partial[:held] + near.astype(wide)
        return total + middle.astype(wide) + far.astype(wide)
    parts = [partial[j * held : (j + 1) * held] for j in range(count)]
    total = parts[0]
    for by in (1, -1):
        carried = None
        for far in range(count - 1, 0, -1):
            own = parts[(-far * by) % count]
            if carried is not None:
                own = own + carried.astype(wide)
            first, last = (0, count - far) if by == 1 else (far, count)
            pairs = [(i, i + by) for i in range(first, last)]
            carried = lax.ppermute(own.astype(low), "tensor", pairs)
        if carried is not None:
            total = total + carried.astype(wide)
    return total


def rotated(value, by):
    count = lax.axis_size("section")
    return lax.ppermute(value, "section", [(i, (i + by) % count) for i in range(count)])


def mirrored(value):
    count = lax.axis_size("section")
    return lax.ppermute(value, "section", [(i, count - 1 - i) for i in range(count)])


def gelu_with_slope(preact):
    tanh_input = tanh_scale * (preact + cubic_term * preact * preact * preact)
    tangent = jnp.tanh(tanh_input)
    values = 0.5 * preact * (1.0 + tangent)
    slopes = 0.5 * (1.0 + tangent) + 0.5 * preact * (1.0 - tangent * tangent) * tanh_scale * (
        1.0 + 3.0 * cubic_term * preact * preact
    )
    return (values, slopes)


def normalize(inputs):
    widened = inputs.astype(wide)
    centred = widened - jnp.mean(widened, axis=-1, keepdims=True)
    inverse_scale = lax.rsqrt(jnp.mean(centred * centred, axis=-1, keepdims=True) + epsilon)
    return (centred * inverse_scale, inverse_scale)


def dot(left, right, left_dim, right_dim):
    dims = (((left_dim,), (right_dim,)), ((), ()))
    return lax.dot_general(left, right, dims, preferred_element_type=wide)


def hidden_kernel(layout, held, scales, places, *refs):
    step = pl.program_id(0)
    count = len(layout) // 2
    loads = sum(layout)
    first, second, hidden, partial, beside, leaving, rows, cotans = refs[loads:]
    model_scale, hidden_scale = scales

    @pl.when(step == 0)
    def _():
        at = 0
        for number, choices in enumerate(layout):
            target = rows if number < count else cotans
            span = pl.ds(number % count * held, held)

            def place(ref, target=target, span=span):
                target[span, :] = ref[...]

            if choices == 1:
                place(refs[at])
            else:
                pl.when(places[0] == 1)(functools.partial(place, refs[at]))
                pl.when(places[0] == 0)(functools.partial(place, refs[at + 1]))
            at += choices

    preact = dot(rows[...], first[0], 1, 0) * model_scale
    values, slopes = gelu_with_slope(preact)
    grad_activation = dot(cotans[...], second[0], 1, 1) * hidden_scale
    grad_preact = (grad_activation * slopes).astype(low)
    hidden[0] = grad_preact
    hidden[1] = values.astype(low)
    term = dot(grad_preact, first[0], 1, 1) * model_scale

    @pl.when(step == 0)
    def _():
        partial[...] = term

    @pl.when(step > 0)
    def _():
        partial[...] += term

    @pl.when(step == pl.num_programs(0) - 1)
    def _():
        beside[...] = partial[held : 2 * held, :].astype(low)
        leaving[...] = partial[2 * held :, :].astype(low)


def hidden_layer(row_blocks, cotan_blocks, held, first, second, keep):
    count = len(row_blocks)
    width, mine = first.shape[1:]
    tile = min(256, mine)
    total = count * held
    scales = (width**-0.5, (mine * count) ** -0.5)
    places = is_central().astype(jnp.int32).reshape(1)
    operands, specs, layout = [], [], []
    for slot, part in row_blocks + cotan_blocks:
        slot = slot if isinstance(slot, tuple) else (slot,)
        operands += slot
        specs += [pl.BlockSpec((held, width), lambda j, at, part=part: (part, 0))] * len(slot)
        layout.append(len(slot))
    specs.append(pl.BlockSpec((1, width, tile), lambda j, at: (0, 0, j)))
    specs.append(pl.BlockSpec((1, tile, width), lambda j, at: (0, j, 0)))
    whole_rows = pl.BlockSpec((total, width), lambda j, at: (0, 0))
    out_specs = [
        pl.BlockSpec((2, total, tile), lambda j, at: (0, 0, j)),
        whole_rows,
        pl.BlockSpec((held, width), lambda j, at: (0, 0)),
        pl.BlockSpec((total - 2 * held, width), lambda j, at: (0, 0)),
    ]
    shapes = [
        jax.ShapeDtypeStruct((2, total, mine), low),
        jax.ShapeDtypeStruct((total, width), wide),
        jax.ShapeDtypeStruct((held, width), low),
        jax.ShapeDtypeStruct((total - 2 * held, width), low),
    ]
    scratch = [pltpu.VMEM((total, width), low)] * 2
    if keep:
        out_specs += [whole_rows] * 2
        shapes += [jax.ShapeDtypeStruct((total, width), low)] * 2
        scratch = []
    return pl.pallas_call(
        functools.partial(hidden_kernel, tuple(layout), held, scales),
        out_shape=shapes,
        grid_spec=pltpu.PrefetchScalarGridSpec(
            num_scalar_prefetch=1,
            grid=(mine // tile,),
            in_specs=specs,
            out_specs=out_specs,
            scratch_shapes=scratch,
        ),
        cost_estimate=pl.CostEstimate(
            flops=6 * total * width * mine,
            bytes_accessed=4 * width * mine + 20 * total * width,
            transcendentals=total * mine,
        ),
    )(places, *operands, first, second)


def update_kernel(lefts, rights, scale, loads, *refs):
    step = pl.program_id(0)
    momentum, weight, fresh, moved, *stacks = refs[loads:]

    def piece(ref, start, length):
        ref = refs[ref]
        if len(ref.shape) == 3:
            return ref[0, start : start + length, :]
        return ref[start : start + length, :]

    sums = []
    for term in range(4):
        sides = []
        for side, parts in enumerate((lefts[term], rights[term])):
            if len(parts) == 1:
                sides.append(piece(*parts[0]))
                continue
            stack = stacks[term % 2]

            def pile(stack=stack, parts=parts):
                at = 0
                for part in parts:
                    stack[at : at + part[2], :] = piece(*part)
                    at += part[2]

            if side:
                pl.when(step == 0)(pile)
            else:
                pile()
            sides.append(stack[...])
        sums.append(dot(sides[0], sides[1], 0, 0))
    down = (sums[0] + sums[1]) * scale
    up = ((sums[2] + sums[3]) * scale).astype(low).astype(wide)
    moment = momentum_decay * momentum[0].astype(wide) + (down + up)
    fresh[0] = (weight[0].astype(wide) - learning_rate * moment).astype(low)
    moved[0] = moment.astype(low)


def update(lefts, rights, scale, momentum, weight):
    depth, breadth = weight.shape[1:]
    tile = min(256, depth)
    operands, specs, seen = [], [], {}
    total = sum(part[3] for part in lefts[0])

    def listed(sides, tiled):
        terms = []
        for parts in sides:
            term = []
            for array, plane, start, length in parts:
                key = (id(array), plane, tiled)
                if key not in seen:
                    seen[key] = len(operands)
                    operands.append(array)
                    columns = tile if tiled else breadth
                    shape = (array.shape[-2], columns)
                    if plane is None:
                        index = (lambda i: (0, i)) if tiled else (lambda i: (0, 0))
                    else:
                        shape = (1, *shape)
                        index = (
                            (lambda i, plane=plane: (plane, 0, i))
                            if tiled
                            else (lambda i, plane=plane: (plane, 0, 0))
                        )
                    specs.append(pl.BlockSpec(shape, index))
                term.append((seen[key], start, length))
            terms.append(tuple(term))
        return tuple(terms)

    left_terms = listed(lefts, True)
    right_terms = listed(rights, False)
    loads = len(operands)
    columns = tile if len(left_terms[2]) > 1 else breadth
    block = pl.BlockSpec((1, tile, breadth), lambda i: (0, i, 0))
    return pl.pallas_call(
        functools.partial(update_kernel, left_terms, right_terms, scale, loads),
        out_shape=[jax.ShapeDtypeStruct(weight.shape, low)] * 2,
        grid=(depth // tile,),
        in_specs=[*specs, block, block],
        out_specs=[block, block],
        scratch_shapes=[pltpu.VMEM((total, columns), low)] * 2,
        cost_estimate=pl.CostEstimate(
            flops=8 * total * depth * breadth,
            bytes_accessed=8 * depth * breadth + 8 * total * (depth + breadth),
            transcendentals=0,
        ),
    )(*operands, momentum, weight)


def input_gradient(grad_normed, normed, inverse_scale, cotan):
    first_mean = jnp.mean(grad_normed, axis=-1, keepdims=True)
    second_mean = jnp.mean(grad_normed * normed, axis=-1, keepdims=True)
    return (
        cotan.astype(wide) + inverse_scale * (grad_normed - first_mean - normed * second_mean)
    ).astype(low)


def body(
    inputs_down,
    inputs_up,
    grads_down,
    grads_up,
    loss_grads,
    first_down,
    second_down,
    first_up,
    second_up,
    momentum_first,
    momentum_second,
):
    sections = lax.axis_size("section")
    position = lax.axis_index("section")
    count = lax.axis_size("tensor")
    rows = grads_down.shape[1]
    held = rows + (-rows) % 8
    width, mine = first_down.shape[1:]

    def padded(value):
        return jnp.pad(value, ((0, held - rows), (0, 0)))

    firsts = (first_up, first_down)
    seconds = (second_up, second_down)
    inputs = (inputs_up[0], inputs_down[0])
    cotans = [padded(grads_up[0]), padded(grads_down[0])]
    losses = (padded(loss_grads[1]), padded(loss_grads[0]))
    edges = (sections - 1, 0)
    ways = (1, -1)
    normed = [[normalize(padded(inputs[b][s])) for s in range(2)] for b in range(2)]
    lows = [[normed[b][s][0].astype(low) for s in range(2)] for b in range(2)]

    def together(*values):
        return jnp.concatenate(values, axis=0)

    def move_on(b, passed):
        value = jnp.where(position == edges[b], losses[b], passed)
        return rotated(value, ways[b])

    def hidden(b, row_slots, cotan_slots, part):
        row_blocks = [(slot, 0) for slot in row_slots]
        cotan_blocks = [(slot, part) for slot in cotan_slots]
        return hidden_layer(row_blocks, cotan_blocks, held, firsts[b], seconds[b], bool(b))

    def grown(b, step, terms):
        total = reduce_line(*terms[1:4])
        return input_gradient(total, *normed[b][step], cotans[b])

    def far_slots(slots):
        rest = mirrored(together(*[chosen(slot) for slot in slots[2:]]))
        return mirrored(slots[0]), mirrored(slots[1]), rest

    up_slots = gather_line(together(lows[0][0], cotans[0]))
    down_slots = gather_line(together(lows[1][0], cotans[1]))
    up_next = gather_line(lows[0][1])
    down_next = gather_line(lows[1][1])
    far_one = far_slots(up_slots)
    far_next = far_slots(up_next)

    up_one = hidden(0, up_slots, up_slots, 1)
    far_hidden = mirrored(up_one[0])
    cotans[0] = move_on(0, grown(0, 0, up_one))

    down_one = hidden(1, down_slots, down_slots, 1)
    down_passed = grown(1, 0, down_one)
    up_cotans = gather_line(cotans[0])
    cotans[1] = move_on(1, down_passed)
    far_cotan = far_slots(up_cotans)

    up_two = hidden(0, up_next, up_cotans, 0)
    far_preact = mirrored(up_two[0][0])
    far_activation = mirrored(up_two[0][1])
    passed_up = grown(0, 1, up_two)

    down_cotans = gather_line(cotans[1])
    down_two = hidden(1, down_next, down_cotans, 0)
    passed_down = grown(1, 1, down_two)

    total = count * held

    def both_pieces(part):
        pieces = [(slot, None, part * held, held) for slot in far_one[:2]]
        for j in range(count - 2):
            pieces.append((far_one[2], None, (2 * j + part) * held, held))
        return pieces

    def plain_pieces(slots):
        pieces = [(slot, None, 0, held) for slot in slots[:2]]
        return [*pieces, (slots[2], None, 0, total - 2 * held)]

    first_new, momentum_one = update(
        [
            [(down_one[4], None, 0, total)],
            [(down_two[4], None, 0, total)],
            both_pieces(0),
            plain_pieces(far_next),
        ],
        [
            [(down_one[0], 0, 0, total)],
            [(down_two[0], 0, 0, total)],
            [(far_hidden, 0, 0, total)],
            [(far_preact, None, 0, total)],
        ],
        width**-0.5,
        momentum_first,
        first_down,
    )
    second_new, momentum_two = update(
        [
            [(down_one[0], 1, 0, total)],
            [(down_two[0], 1, 0, total)],
            [(far_hidden, 1, 0, total)],
            [(far_activation, None, 0, total)],
        ],
        [
            [(down_one[5], None, 0, total)],
            [(down_two[5], None, 0, total)],
            both_pieces(1),
            plain_pieces(far_cotan),
        ],
        (mine * count) ** -0.5,
        momentum_second,
        second_down,
    )
    return (
        first_new,
        second_new,
        momentum_one,
        momentum_two,
        passed_down[:rows][None],
        passed_up[:rows][None],
    )


def solution(mesh):
    placed = (
        P("section", None, "tensor", None),
        P("section", None, "tensor", None),
        P("section", "tensor", None),
        P("section", "tensor", None),
        P(None, "tensor", None),
        P("section", None, "tensor"),
        P("section", "tensor", None),
        P("section", None, "tensor"),
        P("section", "tensor", None),
        P("section", None, "tensor"),
        P("section", "tensor", None),
    )

    return jax.shard_map(
        body,
        mesh=mesh,
        in_specs=placed,
        out_specs=(
            P("section", None, "tensor"),
            P("section", "tensor", None),
            P("section", None, "tensor"),
            P("section", "tensor", None),
            P("section", "tensor", None),
            P("section", "tensor", None),
        ),
        check_vma=False,
    )
```
